32 devices in a mesh: azim: 8 (over y, x, core), axial: 4 (over z).
Axes of the slice: x: 2, y: 2, z: 4, core: 2. Of those that a mesh axis runs over, the one named last changes fastest.
Arguments:
- field: bfloat16 [2, 4, 128, 1024], P(None, None, 'axial', 'azim'), may hold values from -6 to 6
- near_tiles: bfloat16 [2, 16, 64, 2, 128, 128], P(None, 'axial', 'azim'), may hold values from -0.25 to 0.25
- near_pick: int32 [16, 64, 2], P('axial', 'azim'), may hold values from 0 to 48, all different within a row
- factors: bfloat16 [4, 8, 5, 4, 128, 128], P('axial', 'azim'), may hold values from -0.25 to 0.25
Outputs:
- scattered: float32 [2, 4, 128, 1024], P(None, None, 'axial', 'azim')
The draws below stay inside these ranges and needn't reach their ends.
Inputs may be any that keep to these rules, and one draw needn't show every extreme that they name: `near_pick`: each tile names 2 different offsets within the square of 7**2 tile offsets.
All inputs are finite; a program needn't handle non-finite values.
Results may differ from the reference program's by a relative error of at most 0.0045.
Values may be sent and summed in bfloat16 or wider, within the bound.
A program may use at most 64 MiB of HBM per device.

```python
import jax
import jax.numpy as jnp
import numpy as np
from jax import lax

ANG = 4
TX = 8
TZ = 16
REACH = 3
KNEAR = 2
LEVELS = 5
CAX = 32
CAZ = 128
K = 128
AXL = 128
AZM = 1024
TILES_AX = 16
TILES_AZ = 64
NOFF = 49
DEV_AX = 4
DEV_AZ = 8
N_AZIM = 8
N_AXIAL = 4


def block_scale(own_key, extent, pieces, smallest, high):
    factor_of = 1.0
    for position, blocks in pieces:
        steps = jax.random.uniform(jax.random.fold_in(jax.random.fold_in(own_key, 6), position), (blocks,), jnp.float32, smallest / len(pieces), high / len(pieces))
        factor_of = factor_of * jnp.repeat(jnp.exp(steps), extent[position] // blocks).reshape((-1,) + (1,) * (len(extent) - 1 - position))
    return factor_of


def choose_distinct(rng, rows, number_of, top, lift):
    sequence = jax.random.permutation(jax.random.fold_in(rng, 1), number_of)
    pull = sequence
    for power in range(3):
        pull = pull * pull // number_of
    pull = pull * lift // number_of
    lots = jax.random.randint(jax.random.fold_in(rng, 2), (rows, number_of), 0, 4096) + pull
    fixed_rows = jax.random.permutation(jax.random.fold_in(rng, 3), rows)[jnp.arange(number_of) % rows]
    lots = jnp.where(jnp.arange(rows)[:, None] == fixed_rows[None, :], 1 << 14, lots)
    merit = lots * number_of + jnp.arange(number_of)
    return lax.top_k(merit.astype(jnp.int32), top)[1].astype(jnp.int32)


def noise(own_key, shape, width, bound, pieces=(), kind=jnp.bfloat16):
    values = width * jax.random.normal(own_key, shape, jnp.float32)
    if pieces:
        values = values * block_scale(own_key, shape, pieces, -0.22, 0.18)
    return jnp.clip(values, -bound, bound).astype(kind)


def setup_inputs(seed: int = 0) -> dict:
    streams_of = jax.random.split(jax.random.key(seed), 5)
    return {
        "field": noise(streams_of[0], (2, ANG, AXL, AZM), 1.0, 6.0, ((2, 4), (3, 8))),
        "near_tiles": noise(streams_of[1], (2, TILES_AX, TILES_AZ, KNEAR, K, K), (2 * KNEAR * K) ** -0.5, 0.25, ((1, 4), (2, 8))),
        "near_pick": choose_distinct(streams_of[2], TILES_AX * TILES_AZ, NOFF, KNEAR, 0).reshape((TILES_AX, TILES_AZ, KNEAR)),
        "factors": noise(streams_of[3], (DEV_AX, DEV_AZ, LEVELS, 4, K, K), (4 * K) ** -0.5, 0.25, ((0, 4), (1, 8))),
    }


def tile_view(grid):
    lead = grid.shape[:2]
    rows, cols = grid.shape[2], grid.shape[3]
    shaped = grid.reshape(lead + (rows // TX, TX, cols // TZ, TZ))
    return shaped.transpose(0, 1, 2, 4, 3, 5).reshape(lead + (rows // TX, cols // TZ, TX * TZ))


def grid_view(tiles):
    lead = tiles.shape[:2]
    trows, tcols = tiles.shape[2], tiles.shape[3]
    shaped = tiles.reshape(lead + (trows, tcols, TX, TZ))
    return shaped.transpose(0, 1, 2, 4, 3, 5).reshape(lead + (trows * TX, tcols * TZ))


def combine(weights, own, other):
    own32 = own.astype(jnp.float32)
    other32 = other.astype(jnp.float32)
    w32 = weights.astype(jnp.float32)
    self_terms = jnp.einsum('fon,qatzn->fqatzo', w32[0:2], own32)
    other_terms = jnp.einsum('fon,qatzn->fqatzo', w32[2:4], other32)
    real_part = self_terms[0, 0] - self_terms[1, 1] + other_terms[0, 0] - other_terms[1, 1]
    imag_part = self_terms[0, 1] + self_terms[1, 0] + other_terms[0, 1] + other_terms[1, 0]
    return jnp.stack([real_part, imag_part])


def near_field(field, near_tiles, near_pick):
    rim_x = REACH * TX
    rim_z = REACH * TZ
    span = 2 * REACH + 1
    wrapped = jnp.concatenate([field[..., -rim_z:], field, field[..., :rim_z]], axis=3)
    padded = jnp.pad(wrapped, ((0, 0), (0, 0), (rim_x, rim_x), (0, 0)))
    tiles = tile_view(padded)
    row_base = jnp.arange(TILES_AX, dtype=jnp.int32)[:, None, None]
    col_base = jnp.arange(TILES_AZ, dtype=jnp.int32)[None, :, None]
    rows = row_base + near_pick // span
    cols = col_base + near_pick % span
    sources = tiles[:, :, rows, cols, :]

    def one_row(pair):
        coeffs, inputs = pair
        prod = jnp.einsum('pzkcs,qazks->pqazc', coeffs.astype(jnp.float32), inputs.astype(jnp.float32))
        return jnp.stack([prod[0, 0] - prod[1, 1], prod[0, 1] + prod[1, 0]])

    rows_out = lax.map(one_row, (jnp.moveaxis(near_tiles, 1, 0), jnp.moveaxis(sources, 2, 0)))
    return jnp.moveaxis(rows_out, 0, 2)


def far_field(field, factors):
    tiles = tile_view(field)
    tad = CAX // TX
    tzd = CAZ // TZ
    shaped = tiles.reshape((2, ANG, N_AXIAL, tad, N_AZIM, tzd, K))
    coeffs = shaped.transpose(2, 4, 0, 1, 3, 5, 6)
    top = N_AZIM.bit_length() - 1
    plan = [(1, top - 1), (1, top - 2), (1, 0), (0, 1), (0, 0)]
    both = jax.vmap(jax.vmap(combine))
    for level in range(LEVELS):
        axis_pos, bit = plan[level]
        if axis_pos == 1:
            order = np.arange(N_AZIM) ^ (1 << bit)
            partner = coeffs[:, order]
        else:
            order = np.arange(N_AXIAL) ^ (1 << bit)
            partner = coeffs[order]
        result = both(factors[:, :, level], coeffs, partner)
        if level < LEVELS - 1:
            coeffs = result.astype(jnp.bfloat16)
        else:
            coeffs = result
    back = coeffs.transpose(2, 3, 0, 4, 1, 5, 6)
    return back.reshape((2, ANG, TILES_AX, TILES_AZ, K))


def reference(field, near_tiles, near_pick, factors):
    near = near_field(field, near_tiles, near_pick)
    far = far_field(field, factors)
    return grid_view(near + far)
```

```python
import functools

import jax
import jax.numpy as jnp
from jax import lax
from jax.experimental import pallas as pl
from jax.experimental.pallas import tpu as pltpu
from jax.sharding import PartitionSpec as P

TX = 8
TZ = 16
REACH = 3
SPAN = 2 * REACH + 1
F32 = jnp.float32
BF16 = jnp.bfloat16


def swap_groups(parts):
    lanes = len(parts) * TZ
    group = lax.broadcasted_iota(jnp.int32, parts[0].shape, 1) // TZ
    bit = len(parts) // 2
    while bit:
        high = (group & bit) != 0
        swapped = list(parts)
        for i in range(len(parts)):
            if i & bit == 0:
                low_part, high_part = parts[i], parts[i | bit]
                swapped[i] = jnp.where(high, pltpu.roll(high_part, bit * TZ, 1), low_part)
                swapped[i | bit] = jnp.where(
                    high, high_part, pltpu.roll(low_part, lanes - bit * TZ, 1)
                )
        parts = swapped
        bit //= 2
    return parts


def complex_fold(both, width):
    by_re, by_im = both[:, :width], both[:, width:]
    rows = both.shape[0]
    turned = pltpu.roll(by_im.reshape(rows // 8, 8, width), 4, 1).reshape(rows, width)
    row = lax.broadcasted_iota(jnp.int32, (rows, width), 0)
    return by_re + jnp.where((row & 4) == 0, -turned, turned)


def times(left, right):
    return lax.dot_general(
        left, right, (((1,), (1,)), ((), ())), preferred_element_type=F32
    )


def kernel(
    dims,
    pick_hbm,
    field_hbm,
    near_hbm,
    factors_hbm,
    out_ref,
    pick_ref,
    field_vm,
    wide,
    near_vm,
    weights,
    mate_weights,
    pad,
    near_sum,
    start,
    held,
    arrived,
    last,
    last_arrived,
    pick_sem,
    field_sem,
    near_sem,
    factor_sem,
    send_sem,
    recv_sem,
    mate_send,
    mate_recv,
    halo_send,
    halo_recv,
):
    azim_count, axial_count, plan, trows, tcols, lead, order = dims
    d = lax.axis_index("azim")
    e = lax.axis_index("axial")
    rows = trows * tcols * lead
    half = rows // 2

    def xor(value, bit):
        return value + (1 << bit) * (1 - 2 * ((value // (1 << bit)) % 2))

    partners = []
    for level, bit in enumerate(plan):
        if level < 3:
            partners.append({"azim": xor(d, bit), "axial": e})
        else:
            partners.append({"azim": d, "axial": xor(e, bit)})
    side = d % 2
    mate_d = xor(d, 0)
    mate = {"azim": mate_d, "axial": e}
    mine = pl.ds(pl.multiple_of(side * half, half), half)
    theirs = pl.ds(pl.multiple_of((1 - side) * half, half), half)
    cross = {"azim": xor(xor(d, plan[0]), 0), "axial": e}
    reached = sorted(1 << bit for bit in plan[:3]) == [1, 2, 4] and azim_count == 8
    right = (d + 1) % azim_count
    left = (d + azim_count - 1) % azim_count
    has_up = e > 0
    has_down = e < axial_count - 1

    barrier = pltpu.get_barrier_semaphore()

    def greet(device):
        pl.semaphore_signal(
            barrier, inc=1, device_id=device, device_id_type=pl.DeviceIdType.MESH
        )

    for partner in (partners[0], cross, partners[1], mate):
        greet(partner)
    if not reached:
        for column in (left, right):
            greet({"azim": column, "axial": e})

    @pl.when(has_up)
    def _():
        greet({"azim": d, "axial": e - 1})

    @pl.when(has_down)
    def _():
        greet({"azim": d, "axial": e + 1})

    field_copy = pltpu.make_async_copy(field_hbm, field_vm, field_sem)
    field_copy.start()
    factor_copy = pltpu.make_async_copy(factors_hbm.at[0, 0], weights, factor_sem)
    factor_copy.start()
    near_copies = [
        pltpu.make_async_copy(near_hbm.at[:, r], near_vm.at[:, r], near_sem.at[r])
        for r in range(trows)
    ]
    pick_copy = pltpu.make_async_copy(pick_hbm, pick_ref, pick_sem)
    pick_copy.start()

    own_c = slice(REACH, REACH + tcols)

    @pl.when(jnp.logical_not(has_up))
    def _():
        pad[0:REACH, own_c] = jnp.zeros((REACH, tcols) + pad.shape[2:], BF16)

    @pl.when(jnp.logical_not(has_down))
    def _():
        pad[REACH + trows :, own_c] = jnp.zeros((REACH, tcols) + pad.shape[2:], BF16)

    field_copy.wait()
    wide[...] = field_vm[...].astype(F32)
    for r in range(trows):
        parts = [wide[pl.ds(r * TX + i, lead, stride=trows * TX), :] for i in range(TX)]
        tiles = swap_groups(parts)
        for c in range(tcols):
            pad[REACH + r, REACH + c] = tiles[c].astype(BF16)
        base = r * tcols * lead
        start[base : base + tcols * lead, :] = jnp.concatenate(tiles, axis=0).astype(BF16)

    edges = (e == 0).astype(jnp.int32) + (e == axial_count - 1).astype(jnp.int32)
    if reached:
        pl.semaphore_wait(barrier, 6 - edges)
    else:
        pl.semaphore_wait(barrier, 8 - edges)

    def remote(src, dst, sems, index, device):
        return pltpu.make_async_remote_copy(
            src_ref=src,
            dst_ref=dst,
            send_sem=sems[0].at[index],
            recv_sem=sems[1].at[index],
            device_id=device,
            device_id_type=pl.DeviceIdType.MESH,
        )

    pair_sems, mate_sems = (send_sem, recv_sem), (mate_send, mate_recv)
    axial_mate = {"azim": mate_d, "axial": partners[4]["axial"]}
    exchanges = {
        0: [
            remote(start.at[mine], arrived.at[0, 0], pair_sems, (0, 0), partners[0]),
            remote(start.at[theirs], arrived.at[0, 1], pair_sems, (0, 1), cross),
        ],
        4: [
            remote(last.at[mine], last_arrived.at[mine], pair_sems, (4, 0), partners[4]),
            remote(held.at[4, 1], last_arrived.at[mine], pair_sems, (4, 1), axial_mate),
        ],
    }
    for level in (1, 3):
        exchanges[level] = [
            remote(
                held.at[level, role],
                arrived.at[level, role],
                pair_sems,
                (level, role),
                partners[level],
            )
            for role in range(2)
        ]
    first_half = remote(start.at[theirs], held.at[0, 1], mate_sems, 0, mate)
    last_half = remote(held.at[4, 1], last.at[mine], mate_sems, 1, mate)
    factor_sends = [
        remote(weights.at[level], mate_weights.at[level], mate_sems, 2 + level, mate)
        for level in range(len(plan) - 1)
    ]

    for copy in exchanges[0]:
        copy.start()
    first_half.start()
    factor_copy.wait()
    for copy in factor_sends:
        copy.start()
    for copy in near_copies:
        copy.start()

    def halo(index, src_rows, src_cols, dst_row, dst_col, device):
        count_r, count_c = src_rows[1] - src_rows[0], src_cols[1] - src_cols[0]
        return pltpu.make_async_remote_copy(
            src_ref=pad.at[
                pl.ds(REACH + src_rows[0], count_r), pl.ds(REACH + src_cols[0], count_c)
            ],
            dst_ref=pad.at[pl.ds(dst_row, count_r), pl.ds(dst_col, count_c)],
            send_sem=halo_send.at[index],
            recv_sem=halo_recv.at[index],
            device_id=device,
            device_id_type=pl.DeviceIdType.MESH,
        )

    every_c = (0, tcols)
    whole_r = (-REACH, trows + REACH)
    head_c, tail_c = (0, REACH), (tcols - REACH, tcols)
    past_r, past_c = REACH + trows, REACH + tcols
    level_halos = [
        halo(0, whole_r, tail_c, 0, 0, {"azim": right, "axial": e}),
        halo(1, whole_r, head_c, 0, past_c, {"azim": left, "axial": e}),
    ]
    down_halo = halo(2, (trows - REACH, trows), every_c, 0, REACH, {"azim": d, "axial": e + 1})
    up_halo = halo(3, (0, REACH), every_c, past_r, REACH, {"azim": d, "axial": e - 1})

    @pl.when(has_down)
    def _():
        down_halo.start()

    @pl.when(has_up)
    def _():
        up_halo.start()

    def met_axial():
        @pl.when(has_up)
        def _():
            down_halo.wait_recv()

        @pl.when(has_down)
        def _():
            up_halo.wait_recv()

    def near_field():
        for copy in level_halos:
            copy.wait_recv()
        pick_copy.wait()
        for copy in near_copies:
            copy.wait()

        width = near_vm.shape[-1]

        def tile_row(r, carry):
            for c in range(tcols):
                sources = []
                for k in range(near_vm.shape[3]):
                    offset = pick_ref[r, k, c]
                    row = r + lax.div(offset, SPAN)
                    column = c + lax.rem(offset, SPAN)
                    sources.append(pad[row, column])
                blocks = jnp.concatenate(
                    [
                        near_vm[:, r, c, k].reshape(2 * width, width)
                        for k in range(near_vm.shape[3])
                    ],
                    axis=1,
                )
                both = times(jnp.concatenate(sources, axis=1), blocks)
                at = pl.multiple_of((r * tcols + c) * lead, lead)
                near_sum[pl.ds(at, lead), :] = complex_fold(both, width)
            return carry

        lax.fori_loop(0, trows, tile_row, 0)

    width = weights.shape[-1]
    by_role = (weights, mate_weights)

    def block(ref, level, which):
        return ref[level, 2 * which : 2 * which + 2].reshape(2 * width, width)

    def joined(own, level, role):
        both = own + times(arrived[level, role], block(by_role[role], level, 1))
        return complex_fold(both, width)

    own = [times(start[mine, :], block(weights, 0, 0))]
    first_half.wait_recv()
    factor_sends[0].wait_recv()
    own.append(times(held[0, 1], block(mate_weights, 0, 0)))
    for role in range(2):
        exchanges[0][role].wait_recv()
        held[1, role] = joined(own[role], 0, role).astype(BF16)
        exchanges[1][role].start()
    factor_sends[1].wait_recv()
    own = [times(held[1, role], block(by_role[role], 1, 0)) for role in range(2)]
    factor_sends[2].wait_recv()
    met_axial()
    for copy in exchanges[1]:
        copy.wait_recv()
    coeffs = [joined(own[role], 1, role).astype(BF16) for role in range(2)]

    for role in range(2):
        both = times(coeffs[role], block(by_role[role], 2, 0)) + times(
            coeffs[1 - role], block(by_role[role], 2, 1)
        )
        held[3, role] = complex_fold(both, width).astype(BF16)
        exchanges[3][role].start()
    for copy in level_halos:
        copy.start()

    factor_sends[3].wait_recv()
    own = [times(held[3, role], block(by_role[role], 3, 0)) for role in range(2)]
    exchanges[3][0].wait_recv()
    last[mine, :] = joined(own[0], 3, 0).astype(BF16)
    exchanges[4][0].start()
    exchanges[3][1].wait_recv()
    held[4, 1] = joined(own[1], 3, 1).astype(BF16)
    exchanges[4][1].start()
    last_half.start()

    near_field()
    near_sum[mine, :] += complex_fold(times(last[mine, :], block(weights, 4, 0)), width)
    last_half.wait_recv()
    near_sum[theirs, :] += complex_fold(times(last[theirs, :], block(weights, 4, 0)), width)
    for copy in exchanges[4]:
        copy.wait_recv()
    per = tcols * lead
    for j, part in enumerate((mine, theirs)):
        both = times(last_arrived[part, :], block(weights, 4, 1))
        total = complex_fold(both, width) + near_sum[part, :]
        first = (side if j == 0 else 1 - side) * (half // per)
        for q in range(half // per):
            parts = swap_groups(
                [
                    total[q * per + c * lead : q * per + (c + 1) * lead]
                    for c in range(tcols)
                ]
            )
            for i in range(TX):
                at = (first + q) * TX + i
                out_ref[pl.ds(at, lead, stride=trows * TX), :] = parts[i]

    for copies in exchanges.values():
        for copy in copies:
            copy.wait_send()
    for copy in [first_half, last_half] + factor_sends:
        copy.wait_send()

    @pl.when(has_down)
    def _():
        down_halo.wait_send()

    @pl.when(has_up)
    def _():
        up_halo.wait_send()

    for copy in level_halos:
        copy.wait_send()


def solution(mesh):
    placed = (
        P(None, None, "axial", "azim"),
        P(None, "axial", "azim", None, None, None),
        P("axial", "azim", None),
        P("axial", "azim", None, None, None, None),
    )
    azim_count, axial_count = mesh.shape["azim"], mesh.shape["axial"]
    top = azim_count.bit_length() - 1
    plan = (top - 1, top - 2, 0, 1, 0)

    def on_device(field, near_tiles, near_pick, factors):
        parts, angles, rows, columns = field.shape
        lead = parts * angles
        trows, tcols = rows // TX, columns // TZ
        cells = TX * TZ
        flat = field.reshape(lead * rows, columns)
        total = trows * tcols * lead
        dims = (azim_count, axial_count, plan, trows, tcols, lead, tuple(mesh.axis_names))
        any_space = pl.BlockSpec(memory_space=pl.ANY)
        out = pl.pallas_call(
            functools.partial(kernel, dims),
            out_shape=pltpu.VMEM((lead * rows, columns), F32),
            in_specs=[any_space] * 4,
            out_specs=pl.BlockSpec(memory_space=pltpu.VMEM),
            scratch_shapes=[
                pltpu.SMEM((trows, near_pick.shape[2], tcols), jnp.int32),
                pltpu.VMEM(flat.shape, BF16),
                pltpu.VMEM(flat.shape, F32),
                pltpu.VMEM(near_tiles.shape, BF16),
                pltpu.VMEM(factors.shape[2:], BF16),
                pltpu.VMEM(factors.shape[2:], BF16),
                pltpu.VMEM((trows + 2 * REACH, tcols + 2 * REACH, lead, cells), BF16),
                pltpu.VMEM((total, cells), F32),
                pltpu.VMEM((total, cells), BF16),
                pltpu.VMEM((len(plan), 2, total // 2, cells), BF16),
                pltpu.VMEM((len(plan), 2, total // 2, cells), BF16),
                pltpu.VMEM((total, cells), BF16),
                pltpu.VMEM((total, cells), BF16),
                pltpu.SemaphoreType.DMA,
                pltpu.SemaphoreType.DMA,
                pltpu.SemaphoreType.DMA((trows,)),
                pltpu.SemaphoreType.DMA,
                pltpu.SemaphoreType.DMA((len(plan), 2)),
                pltpu.SemaphoreType.DMA((len(plan), 2)),
                pltpu.SemaphoreType.DMA((len(plan) + 1,)),
                pltpu.SemaphoreType.DMA((len(plan) + 1,)),
                pltpu.SemaphoreType.DMA((4,)),
                pltpu.SemaphoreType.DMA((4,)),
            ],
            compiler_params=pltpu.CompilerParams(collective_id=0, has_side_effects=True),
        )(near_pick.transpose(0, 2, 1), flat, near_tiles, factors)
        return out.reshape(field.shape)

    return jax.shard_map(
        on_device,
        mesh=mesh,
        in_specs=placed,
        out_specs=P(None, None, "axial", "azim"),
        check_vma=False,
    )
```
